128 devices in a mesh: user: 16 (over y, z), item: 8 (over x, core).
Axes of the slice: x: 4, y: 4, z: 4, core: 2. Of those that a mesh axis runs over, the one named last changes fastest.
Arguments:
- tile_values: bfloat16 [256, 32, 256, 128], P('user', 'item'), may hold values from -600 to 600
- tile_ids: int32 [256, 32], P('user', 'item'), may hold values from 0 to 2047, as said below
- lengths: int32 [256], P('user'), may hold values from 128 to 256
- user_weights: float32 [256, 256], P('user'), may hold values from 0.5 to 16
- time_factor: float32 [256, 256], replicated, may hold values from -0.25 to 2.25
- item_factor: bfloat16 [262144, 256], P(('item', 'user')), may hold values from -0.2421875 to 0.2421875
Outputs:
- slices: bfloat16 [256, 256, 256], P(('user', 'item'))
- new_time: float32 [256, 256], replicated
- new_items: float32 [262144, 256], P(('item', 'user'))
The draws below stay inside these ranges and needn't reach their ends.
Inputs may be any that keep to these rules, and one draw needn't show every extreme that they name: `tile_ids`: slot block i of a user (slots i * 4 to (i + 1) * 4 - 1) names tiles i * 256 to (i + 1) * 256 - 1. Within the slots of 16 users of one index of user in one slot block, all tiles differ, and at most 8 of them lie in one group of 16 tiles (group g: tiles i * 256 + g * 16 onward); in every slot block some group holds exactly 8 of them for every index of user.
All inputs are finite; a program needn't handle non-finite values.
Results may differ from the reference program's by a relative error of at most 0.014.
Values may be sent and summed in bfloat16 or wider, within the bound.
A program may use at most 128 MiB of HBM per device.

```python
import math
import jax
import jax.numpy as jnp
from jax import lax

R = 256
ROWS = 256
TILE = 128
ITEM_TILES_DEV = 256
U_DEV = 16
NT_DEV = 4
NS_STEPS = 6
USERS = 256
SLOTS = 32
ITEM_TILES = 2048
ITEMS = 262144
N_USER = 16
N_ITEM = 8


def draw_tile_ids(key, part):
    block_slots = U_DEV * NT_DEV
    mean_load = block_slots // N_USER
    owned = ITEM_TILES_DEV // N_USER
    key_star, key_order, key_delta, key_offset, key_shuffle = jax.random.split(jax.random.fold_in(key, 11), 5)
    star_owner = jax.random.randint(key_star, (N_ITEM,), 0, N_USER)
    star_owner = star_owner.at[0].set(0).at[N_ITEM - 1].set(N_USER - 1)
    grid_shape = (N_USER, N_ITEM)
    owner_range = jnp.arange(N_USER, dtype=jnp.int32)
    order_score = jax.random.randint(key_order, grid_shape + (N_USER,), 0, 1 << 20) * N_USER + owner_range
    order_score = jnp.where(owner_range == star_owner[None, :, None], -1, order_score)
    pair_order = jnp.argsort(order_score, axis=-1).astype(jnp.int32)
    delta_load = jax.random.randint(key_delta, grid_shape + (N_USER // 2,), 0, mean_load + 1)
    delta_load = delta_load.at[:, :, 0].set(mean_load)
    load_at = jnp.stack([mean_load + delta_load, mean_load - delta_load], axis=-1).reshape(grid_shape + (N_USER,))
    owner_load = jnp.sum((pair_order[..., :, None] == owner_range).astype(jnp.int32) * load_at[..., :, None], axis=-2)
    load_ends = jnp.cumsum(owner_load, axis=-1)
    load_starts = load_ends - owner_load
    sorted_index = jnp.arange(block_slots, dtype=jnp.int32)
    owner_of = jnp.sum((sorted_index[:, None] >= load_ends[..., None, :]).astype(jnp.int32), axis=-1)
    rank_inside = sorted_index - jnp.take_along_axis(load_starts, owner_of, axis=-1)
    offsets = jax.random.randint(key_offset, grid_shape + (N_USER,), 0, owned)
    offsets = jnp.where(owner_range == star_owner[None, :, None], owned - 1, offsets)
    local_tiles = owner_of * owned + (rank_inside + jnp.take_along_axis(offsets, owner_of, axis=-1)) % owned
    shuffle_score = jax.random.randint(key_shuffle, grid_shape + (block_slots,), 0, 1 << 20) * block_slots + sorted_index
    shuffled = jnp.take_along_axis(local_tiles, jnp.argsort(shuffle_score, axis=-1), axis=-1)
    item_base = (jnp.arange(N_ITEM, dtype=jnp.int32) * ITEM_TILES_DEV)[None, :, None]
    global_ids = (shuffled + item_base).reshape(N_USER, N_ITEM, U_DEV, NT_DEV)
    return jnp.transpose(global_ids, (0, 2, 1, 3)).reshape(N_USER * U_DEV, N_ITEM * NT_DEV).astype(jnp.int32)


def draw_lengths(key, part):
    drawn = jax.random.randint(jax.random.fold_in(key, 23), (USERS,), ROWS // 2, ROWS + 1)
    return drawn.at[0].set(ROWS).at[1].set(ROWS // 2).astype(jnp.int32)


def draw_user_weights(key, part):
    base_key = jax.random.fold_in(key, 37)
    base = jnp.exp(jax.random.uniform(base_key, (USERS, R), jnp.float32, math.log(0.5), math.log(1.0)))
    joined = N_USER * N_ITEM
    holder = jnp.arange(USERS, dtype=jnp.int32) // (U_DEV // N_ITEM)
    column = jnp.arange(R, dtype=jnp.int32)
    position = ((holder[:, None] + column[None, :]) % joined).astype(jnp.float32) / (joined - 1)
    return base * jnp.exp(position * math.log(16.0))


def draw_time_factor(key, part):
    key_off, key_diag = jax.random.split(jax.random.fold_in(key, 41), 2)
    off_part = jax.random.uniform(key_off, (R, R), jnp.float32, -0.25, 0.25)
    diag_part = jax.random.uniform(key_diag, (R,), jnp.float32, 1.25, 2.25)
    on_diag = jnp.arange(R, dtype=jnp.int32)[:, None] == jnp.arange(R, dtype=jnp.int32)[None, :]
    return jnp.where(on_diag, diag_part[None, :], off_part).astype(jnp.float32)


def draw_item_factor(key, part):
    key_val, key_row = jax.random.split(jax.random.fold_in(key, 53), 2)
    base_scale = 1.0 / math.sqrt(NT_DEV * N_ITEM * TILE)
    row_scale = jnp.exp(jax.random.uniform(key_row, (ITEMS, 1), jnp.float32, 0.0, math.log(4.0)))
    values = jax.random.normal(key_val, (ITEMS, R), jnp.float32) * row_scale
    values = jnp.clip(values, -15.0, 15.0) * base_scale
    return values.astype(jnp.bfloat16)


def steps_of(key, shape, cuts, least, top_value):
    factor_of = 1.0
    for axis_at, shards_of in cuts:
        steps = jax.random.uniform(jax.random.fold_in(jax.random.fold_in(key, 6), axis_at), (shards_of,), jnp.float32, least / len(cuts), top_value / len(cuts))
        factor_of = factor_of * jnp.repeat(jnp.exp(steps), shape[axis_at] // shards_of).reshape((-1,) + (1,) * (len(shape) - 1 - axis_at))
    return factor_of


def normal_values(stream_key, dims, deviation, bound, shards=(), held_as=jnp.bfloat16):
    factor_of = steps_of(stream_key, dims, shards, -0.22, 0.18) if shards else 1.0
    entries = jax.random.normal(stream_key, dims, jnp.float32) * deviation * factor_of
    return jnp.minimum(jnp.maximum(entries, -bound), bound).astype(held_as)


def setup_inputs(seed: int = 0) -> dict:
    streams_of = jax.random.split(jax.random.key(seed), 7)
    tile_values = normal_values(streams_of[0], (USERS, SLOTS, ROWS, TILE), 100.0, 600.0, ((0, 16), (1, 8)))
    tile_ids = draw_tile_ids(jax.random.fold_in(streams_of[6], 71), 0)
    lengths = draw_lengths(jax.random.fold_in(streams_of[6], 71), 0)
    user_weights = draw_user_weights(jax.random.fold_in(streams_of[6], 71), 0)
    time_factor = draw_time_factor(jax.random.fold_in(streams_of[6], 71), 0)
    item_factor = draw_item_factor(jax.random.fold_in(streams_of[6], 71), 0)
    return dict(tile_values=tile_values, tile_ids=tile_ids, lengths=lengths, user_weights=user_weights, time_factor=time_factor, item_factor=item_factor)


HIGHEST_PRECISION = lax.Precision.HIGHEST
EPSILON = 1e-06

def polar_factor(target):
    norm_scale = jnp.sqrt(jnp.sum(target * target) + EPSILON)
    iterate = target / norm_scale
    for sweep_index in range(NS_STEPS):
        inner_gram = jnp.dot(iterate.T.astype(jnp.float32), iterate.astype(jnp.float32), precision=HIGHEST_PRECISION, preferred_element_type=jnp.float32)
        iterate = 1.5 * iterate - 0.5 * jnp.dot(iterate.astype(jnp.float32), inner_gram.astype(jnp.float32), precision=HIGHEST_PRECISION, preferred_element_type=jnp.float32)
    return iterate

def spd_solve(gram_matrix, right_side):
    chol_lower = jnp.linalg.cholesky(gram_matrix)
    return jax.scipy.linalg.cho_solve((chol_lower, True), right_side.T).T

def reference(tile_values, tile_ids, lengths, user_weights, time_factor, item_factor):
    panel_table = item_factor.reshape(ITEM_TILES, TILE, R)
    live_rows = (jnp.arange(ROWS, dtype=jnp.int32)[None, :] < lengths[:, None]).astype(tile_values.dtype)

    def project(user_block):
        values, tile_list, live_mask, weights = user_block
        masked = values * live_mask[None, :, None]
        panels = panel_table[tile_list]
        projection = jnp.einsum('srt,stc->rc', masked.astype(jnp.float32), panels.astype(jnp.float32), precision=HIGHEST_PRECISION)
        scaled = projection * weights[None, :]
        target = jnp.dot(scaled.astype(jnp.float32), time_factor.T.astype(jnp.float32), precision=HIGHEST_PRECISION, preferred_element_type=jnp.float32)
        polar_one = polar_factor(target)
        user_term = jnp.dot(polar_one.T.astype(jnp.float32), scaled.astype(jnp.float32), precision=HIGHEST_PRECISION, preferred_element_type=jnp.float32)
        return (polar_one, user_term)
    polar_all, user_terms = lax.map(project, (tile_values, tile_ids, live_rows, user_weights))
    time_mttkrp = lax.optimization_barrier(jnp.sum(user_terms, axis=0))
    weight_gram = jnp.dot(user_weights.T.astype(jnp.float32), user_weights.astype(jnp.float32), precision=HIGHEST_PRECISION, preferred_element_type=jnp.float32)
    item_inner = jnp.dot(item_factor.T.astype(jnp.float32), item_factor.astype(jnp.float32), preferred_element_type=jnp.float32)
    time_raw = spd_solve(item_inner * weight_gram, time_mttkrp)
    new_time = time_raw / jnp.sqrt(lax.optimization_barrier(jnp.sum(time_raw * time_raw, axis=0, keepdims=True)) + EPSILON)
    item_gram = jnp.dot(new_time.T.astype(jnp.float32), new_time.astype(jnp.float32), precision=HIGHEST_PRECISION, preferred_element_type=jnp.float32) * weight_gram

    def accumulate(total, user_block):
        values, tile_list, live_mask, weights, polar_one = user_block
        masked = values * live_mask[None, :, None]
        user_maps = (jnp.dot(polar_one.astype(jnp.float32), new_time.astype(jnp.float32), precision=HIGHEST_PRECISION, preferred_element_type=jnp.float32) * weights[None, :]).astype(jnp.bfloat16)
        tile_terms = jnp.einsum('srt,rc->stc', masked.astype(jnp.float32), user_maps.astype(jnp.float32), precision=HIGHEST_PRECISION).astype(jnp.bfloat16)
        return (total.at[tile_list].add(tile_terms.astype(jnp.float32)), None)
    start_total = jnp.zeros((ITEM_TILES, TILE, R), jnp.float32)
    item_mttkrp, _ = lax.scan(accumulate, start_total, (tile_values, tile_ids, live_rows, user_weights, polar_all))
    new_items = spd_solve(item_gram, item_mttkrp.reshape(ITEMS, R))
    return (polar_all.astype(jnp.bfloat16), new_time, new_items)
```

```python
import jax
import jax.numpy as jnp
from jax import lax
from jax.sharding import PartitionSpec as P

NS_STEPS = 6
HIGHEST = lax.Precision.HIGHEST
EPSILON = 1e-06


def polar_batch(target):
    norm_scale = jnp.sqrt(jnp.sum(target * target, axis=(1, 2), keepdims=True) + EPSILON)
    iterate = target / norm_scale
    for _ in range(NS_STEPS):
        gram = jnp.einsum("krc,krd->kcd", iterate, iterate, precision=HIGHEST)
        iterate = 1.5 * iterate - 0.5 * jnp.einsum("krc,kcd->krd", iterate, gram, precision=HIGHEST)
    return iterate


def spd_solve(gram_matrix, right_side):
    chol_lower = jnp.linalg.cholesky(gram_matrix)
    return jax.scipy.linalg.cho_solve((chol_lower, True), right_side.T).T


def body(tile_values, tile_ids, lengths, user_weights, time_factor, item_factor):
    user_count = lax.axis_size("user")
    item_count = lax.axis_size("item")
    item_pos = lax.axis_index("item")
    users_here, slots_user, time_rows, tile_width = tile_values.shape
    rank_size = time_factor.shape[0]
    tiles_owned = item_factor.shape[0] // tile_width
    slot_count = users_here * slots_user
    share_count = users_here // item_count
    flat_ids = (tile_ids - item_pos * (tiles_owned * user_count)).reshape(slot_count)
    live = jnp.arange(time_rows, dtype=jnp.int32)[None, :] < lengths[:, None]
    shard_rows = lax.all_gather(item_factor, "user", axis=0, tiled=True)
    panels = shard_rows.reshape(tiles_owned * user_count, tile_width, rank_size)[flat_ids]
    panels = panels.reshape(users_here, slots_user, tile_width, rank_size)
    partial = jnp.einsum("ksrt,kstc->krc", tile_values, panels, preferred_element_type=jnp.float32)
    partial = jnp.where(live[:, :, None], partial, 0.0)
    share_start = item_pos * share_count
    share_weights = lax.dynamic_slice_in_dim(user_weights, share_start, share_count, 0)
    projection = lax.psum_scatter(partial, "item", scatter_dimension=0, tiled=True)
    scaled = projection * share_weights[:, None, :]
    polar = polar_batch(jnp.einsum("krc,dc->krd", scaled, time_factor, precision=HIGHEST))
    slices = polar.astype(jnp.bfloat16)
    time_term = jnp.einsum("krc,krd->cd", polar, scaled, precision=HIGHEST)
    weight_term = jnp.dot(share_weights.T, share_weights, precision=HIGHEST)
    item_term = jnp.dot(item_factor.T, item_factor, preferred_element_type=jnp.float32)
    sums = lax.psum((time_term, weight_term, item_term), "item")
    time_mttkrp, weight_gram, item_inner = lax.psum(sums, "user")
    polar_all = lax.all_gather(slices, "item", axis=0, tiled=True).astype(jnp.float32)
    time_raw = spd_solve(item_inner * weight_gram, time_mttkrp)
    new_time = time_raw / jnp.sqrt(jnp.sum(time_raw * time_raw, axis=0, keepdims=True) + EPSILON)
    item_gram = jnp.dot(new_time.T, new_time, precision=HIGHEST) * weight_gram
    user_maps = (
        jnp.einsum("krc,cd->krd", polar_all, new_time, precision=HIGHEST) * user_weights[:, None, :]
    )
    user_maps = jnp.where(live[:, :, None], user_maps, 0.0).astype(jnp.bfloat16)
    tile_terms = jnp.einsum(
        "ksrt,krc->kstc", tile_values, user_maps, preferred_element_type=jnp.float32
    ).astype(jnp.bfloat16)
    tile_terms = tile_terms.reshape(slot_count, tile_width * rank_size)
    row_count = tiles_owned * tile_width * user_count
    wanted = jnp.arange(row_count // tile_width, dtype=jnp.int32)
    hits = (flat_ids[None, :] == wanted[:, None]).astype(jnp.bfloat16)
    summed = jnp.dot(hits, tile_terms, preferred_element_type=jnp.float32)
    item_mttkrp = lax.psum_scatter(
        summed.reshape(row_count, rank_size).astype(jnp.bfloat16),
        "user",
        scatter_dimension=0,
        tiled=True,
    ).astype(jnp.float32)
    new_items = spd_solve(item_gram, item_mttkrp)
    return (slices, new_time, new_items)


def solution(mesh):
    in_specs = (
        P("user", "item", None, None),
        P("user", "item"),
        P("user"),
        P("user", None),
        P(),
        P(("item", "user"), None),
    )
    out_specs = (P(("user", "item"), None, None), P(), P(("item", "user"), None))
    return jax.shard_map(body, mesh=mesh, in_specs=in_specs, out_specs=out_specs, check_vma=False)
```

```python
import functools

import jax
import jax.numpy as jnp
from jax import lax
from jax.experimental import pallas as pl
from jax.experimental.pallas import tpu as pltpu
from jax.sharding import PartitionSpec as P

NS_STEPS = 6
HIGHEST = lax.Precision.HIGHEST
EPSILON = 1e-06
F32, BF16 = jnp.float32, jnp.bfloat16
VMEM = pl.BlockSpec(memory_space=pltpu.VMEM)


def send(src, dst, send_sem, recv_sem, **peer):
    return pltpu.make_async_remote_copy(
        src_ref=src,
        dst_ref=dst,
        send_sem=send_sem,
        recv_sem=recv_sem,
        device_id=peer,
        device_id_type=pl.DeviceIdType.MESH,
    )


def places():
    user, item = lax.axis_index("user"), lax.axis_index("item")
    return user // 4, user % 4, item // 2, item % 2, item


def y_peer(y, z, d):
    return ((y + d) % 4) * 4 + z


def z_peer(y, z, d):
    return y * 4 + (z + d) % 4


def greet(y, z, item):
    barrier = pltpu.get_barrier_semaphore()
    for d in range(1, 8):
        pl.semaphore_signal(
            barrier, inc=1, device_id={"item": (item + d) % 8}, device_id_type=pl.DeviceIdType.MESH
        )
    for d in range(1, 4):
        for peer in (y_peer(y, z, d), z_peer(y, z, d)):
            pl.semaphore_signal(
                barrier, inc=1, device_id={"user": peer}, device_id_type=pl.DeviceIdType.MESH
            )
    pl.semaphore_wait(barrier, 13)


def split(a):
    high = a.astype(BF16)
    return high, (a - high.astype(F32)).astype(BF16)


def dot3(a, b, dims):
    contract = ((dims[0],), (dims[1],)), ((), ())
    one = functools.partial(lax.dot_general, dimension_numbers=contract, preferred_element_type=F32)
    return one(a[0], b[0]) + (one(a[0], b[1]) + one(a[1], b[0]))


def rows_of(j):
    return pl.ds(pl.multiple_of(j * 32, 32), 32)


def scatter_start(term, buf, sems, base, item):
    copies = []
    for d in range(1, 8):
        j = (item + d) % 8
        copies.append(
            send(term.at[rows_of(j)], buf.at[item], sems[0].at[base + d], sems[1].at[base + d], item=j)
        )
        copies[-1].start()
    buf[item] = term[rows_of(item)]
    return copies


def share_start(buf, sems, base, at, peer_of, value):
    buf[at] = value
    copies = []
    for d in range(1, 4):
        copies.append(
            send(buf.at[at], buf.at[at], sems[0].at[base + d], sems[1].at[base + d], user=peer_of(d))
        )
        copies[-1].start()
    return copies


def gather_start(full, sems, base, item, value):
    full[rows_of(item)] = value
    copies = []
    for d in range(1, 8):
        part = full.at[rows_of(item)]
        copies.append(
            send(part, part, sems[0].at[base + d], sems[1].at[base + d], item=(item + d) % 8)
        )
        copies[-1].start()
    return copies


def arrive(copies):
    for copy in copies:
        copy.wait_recv()


def total_of(buf, count):
    total = buf[0]
    for n in range(1, count):
        total = total + buf[n]
    return total


def sum_kernel(term, weights, full, all_weights, buf_x, buf_y, buf_z, send_sem, recv_sem):
    sems = (send_sem, recv_sem)
    y, z, _, _, item = places()
    all_weights[y, z] = weights[...]
    greet(y, z, item)
    started = scatter_start(term, buf_x, sems, 0, item)
    wide = []
    for d in range(1, 4):
        mine = all_weights.at[y, z]
        wide.append(
            send(mine, mine, send_sem.at[24 + d], recv_sem.at[24 + d], user=y_peer(y, z, d))
        )
        wide[-1].start()
    arrive(started)
    step = share_start(
        buf_y, sems, 8, y, functools.partial(y_peer, y, z), total_of(buf_x, 8)
    )
    arrive(wide)
    for d in range(1, 4):
        mine = all_weights.at[:, z]
        wide.append(
            send(mine, mine, send_sem.at[28 + d], recv_sem.at[28 + d], user=z_peer(y, z, d))
        )
        wide[-1].start()
    arrive(step)
    started += step
    step = share_start(
        buf_z, sems, 12, z, functools.partial(z_peer, y, z), total_of(buf_y, 4)
    )
    arrive(step)
    started += step
    step = gather_start(full, sems, 16, item, total_of(buf_z, 4))
    arrive(step)
    arrive(wide[3:])
    for copy in started + step + wide:
        copy.wait_send()


def sum_everywhere(term, weights):
    return pl.pallas_call(
        sum_kernel,
        out_shape=(
            jax.ShapeDtypeStruct((256, 256), F32),
            jax.ShapeDtypeStruct((4, 4, 16, 256), F32),
        ),
        in_specs=[VMEM, VMEM],
        out_specs=(VMEM, VMEM),
        scratch_shapes=[
            pltpu.VMEM((8, 32, 256), F32),
            pltpu.VMEM((4, 32, 256), F32),
            pltpu.VMEM((4, 32, 256), F32),
            pltpu.SemaphoreType.DMA((32,)),
            pltpu.SemaphoreType.DMA((32,)),
        ],
        compiler_params=pltpu.CompilerParams(collective_id=0, has_side_effects=True),
        name="sum_everywhere",
    )(term, weights)


def mid_kernel(
    partial,
    weights,
    time_factor,
    inner_inv,
    weight_gram,
    polar_all,
    slices,
    new_time,
    item_gram,
    recv1,
    outgoing,
    relay,
    recv2,
    scaled,
    iterate,
    term,
    full,
    buf_x,
    buf_y,
    buf_z,
    send_sem,
    recv_sem,
):
    sems = (send_sem, recv_sem)
    y, z, x, core, item = places()
    partner = x * 2 + (1 - core)
    right, left = ((x + 1) % 4) * 2 + core, ((x + 3) % 4) * 2 + core
    done = []

    def go(src, dst, n, **peer):
        copy = send(src, dst, send_sem.at[n], recv_sem.at[n], **peer)
        copy.start()
        done.append(copy)
        return copy

    greet(y, z, item)

    def share(d):
        return (((x + d) % 4) * 2 + core) * 2

    def other_share(d):
        return (((x + d) % 4) * 2 + (1 - core)) * 2

    cross = {}
    for d in (2, 1, 3, 0):
        cross[d] = go(partial.at[pl.ds(other_share(d), 2)], recv1.at[d], d, item=partner)
    cross[2].wait_recv()
    outgoing[0] = (partial[share(2)] + recv1[2, 0]).astype(BF16)
    far_right = go(outgoing.at[0], relay.at[0], 4, item=right)
    outgoing[1] = (partial[share(2) + 1] + recv1[2, 1]).astype(BF16)
    far_left = go(outgoing.at[1], relay.at[1], 5, item=left)
    cross[1].wait_recv()
    outgoing[3] = (partial[share(1) + 1] + recv1[1, 1]).astype(BF16)
    near_right = go(outgoing.at[3], recv2.at[0], 6, item=right)
    cross[3].wait_recv()
    outgoing[4] = (partial[share(3)] + recv1[3, 0]).astype(BF16)
    near_left = go(outgoing.at[4], recv2.at[1], 7, item=left)
    far_right.wait_recv()
    outgoing[2] = (partial[share(1)] + recv1[1, 0] + relay[0].astype(F32)).astype(BF16)
    sum_right = go(outgoing.at[2], recv2.at[2], 8, item=right)
    far_left.wait_recv()
    outgoing[5] = (partial[share(3) + 1] + recv1[3, 1] + relay[1].astype(F32)).astype(BF16)
    sum_left = go(outgoing.at[5], recv2.at[3], 9, item=left)
    cross[0].wait_recv()
    for copy in (near_right, near_left, sum_right, sum_left):
        copy.wait_recv()
    factor = split(time_factor[...])
    for k, parts in enumerate(((2, 1), (0, 3))):
        projection = partial[share(0) + k] + recv1[0, k]
        for n in parts:
            projection = projection + recv2[n].astype(F32)
        projection = projection * weights[k]
        scaled[k] = projection
        target = dot3(split(projection), factor, (1, 1))
        norm = jnp.sum(target * target, axis=(0, 1), keepdims=True) + EPSILON
        iterate[k] = target / jnp.sqrt(norm)

    def sweep(_, carry):
        for k in range(2):
            now = iterate[k]
            parts = split(now)
            gram = dot3(parts, parts, (1, 1))
            iterate[k] = 1.5 * now - 0.5 * dot3(split(gram), parts, (1, 0))
        return carry

    lax.fori_loop(0, NS_STEPS, sweep, 0)
    total = None
    for k in range(2):
        polar = iterate[k]
        slices[k] = polar.astype(BF16)
        polar_all[item * 2 + k] = polar.astype(BF16)
        one = dot3(split(polar.T), split(scaled[k]), (1, 0))
        total = one if total is None else total + one
    term[...] = total
    step = scatter_start(term, buf_x, sems, 16, item)
    done.extend(step)
    mine = polar_all.at[pl.ds(item * 2, 2)]
    own_right = go(mine, mine, 48, item=right)
    own_left = go(mine, mine, 49, item=left)
    crossing = [go(mine, mine, 50, item=partner)]
    arrive(step)
    step = share_start(buf_y, sems, 24, y, functools.partial(y_peer, y, z), total_of(buf_x, 8))
    done.extend(step)
    arrive(step)
    step = share_start(buf_z, sems, 28, z, functools.partial(z_peer, y, z), total_of(buf_y, 4))
    done.extend(step)
    own_right.wait_recv()
    hop = polar_all.at[left * 2]
    hop_right = go(hop, hop, 51, item=right)
    own_left.wait_recv()
    hop = polar_all.at[right * 2 + 1]
    hop_left = go(hop, hop, 52, item=left)
    for n, source in ((53, left), (54, right)):
        block = polar_all.at[pl.ds(source * 2, 2)]
        crossing.append(go(block, block, n, item=partner))
    arrive(step)
    step = gather_start(full, sems, 32, item, total_of(buf_z, 4))
    done.extend(step)
    hop_right.wait_recv()
    hop_left.wait_recv()
    block = polar_all.at[pl.ds(share(2), 2)]
    crossing.append(go(block, block, 55, item=partner))
    arrive(step)
    raw = dot3(split(full[...]), split(inner_inv[...]), (1, 0))
    fresh = raw / jnp.sqrt(jnp.sum(raw * raw, axis=0, keepdims=True) + EPSILON)
    new_time[...] = fresh
    item_gram[...] = dot3(split(fresh.T), split(fresh), (1, 0)) * weight_gram[...]
    arrive(crossing)
    for copy in done:
        copy.wait_send()


def middle(partial, weights, time_factor, inner_inv, weight_gram):
    return pl.pallas_call(
        mid_kernel,
        out_shape=(
            jax.ShapeDtypeStruct((16, 256, 256), BF16),
            jax.ShapeDtypeStruct((2, 256, 256), BF16),
            jax.ShapeDtypeStruct((256, 256), F32),
            jax.ShapeDtypeStruct((256, 256), F32),
        ),
        in_specs=[VMEM] * 5,
        out_specs=(VMEM,) * 4,
        scratch_shapes=[
            pltpu.VMEM((4, 2, 256, 256), F32),
            pltpu.VMEM((6, 256, 256), BF16),
            pltpu.VMEM((2, 256, 256), BF16),
            pltpu.VMEM((4, 256, 256), BF16),
            pltpu.VMEM((2, 256, 256), F32),
            pltpu.VMEM((2, 256, 256), F32),
            pltpu.VMEM((256, 256), F32),
            pltpu.VMEM((256, 256), F32),
            pltpu.VMEM((8, 32, 256), F32),
            pltpu.VMEM((4, 32, 256), F32),
            pltpu.VMEM((4, 32, 256), F32),
            pltpu.SemaphoreType.DMA((56,)),
            pltpu.SemaphoreType.DMA((56,)),
        ],
        compiler_params=pltpu.CompilerParams(collective_id=1, has_side_effects=True),
        name="middle",
    )(partial, weights, time_factor, inner_inv, weight_gram)


def spd_inverse(gram):
    lower = jnp.linalg.cholesky(gram)
    return jax.scipy.linalg.cho_solve((lower, True), jnp.eye(gram.shape[0], dtype=F32))


def body(tile_values, tile_ids, lengths, user_weights, time_factor, item_factor):
    user_count = lax.axis_size("user")
    item_count = lax.axis_size("item")
    item_pos = lax.axis_index("item")
    users_here, slots_user, time_rows, tile_width = tile_values.shape
    rank_size = time_factor.shape[0]
    tiles_owned = item_factor.shape[0] // tile_width
    slot_count = users_here * slots_user
    share_count = users_here // item_count
    flat_ids = (tile_ids - item_pos * (tiles_owned * user_count)).reshape(slot_count)
    live = jnp.arange(time_rows, dtype=jnp.int32)[None, :] < lengths[:, None]
    shard_rows = lax.all_gather(item_factor, "user", axis=0, tiled=True)
    item_term = lax.dot_general(
        item_factor, item_factor, (((0,), (0,)), ((), ())), preferred_element_type=F32
    )
    item_inner, all_weights = sum_everywhere(item_term, user_weights)
    all_weights = all_weights.reshape(user_count * users_here, rank_size)
    weight_gram = jnp.dot(all_weights.T, all_weights, precision=HIGHEST)
    inner_inv = spd_inverse(item_inner * weight_gram)
    panels = shard_rows.reshape(tiles_owned * user_count, tile_width, rank_size)[flat_ids]
    panels = panels.reshape(users_here, slots_user, tile_width, rank_size)
    partial = jnp.einsum("ksrt,kstc->krc", tile_values, panels, preferred_element_type=F32)
    partial = jnp.where(live[:, :, None], partial, 0.0)
    share_weights = lax.dynamic_slice_in_dim(user_weights, item_pos * share_count, share_count, 0)
    polar_all, slices, new_time, item_gram = middle(
        partial, share_weights[:, None, :], time_factor, inner_inv, weight_gram
    )
    gram_inv = spd_inverse(item_gram)
    user_maps = (
        jnp.einsum("krc,cd->krd", polar_all.astype(F32), new_time, precision=HIGHEST)
        * user_weights[:, None, :]
    )
    user_maps = jnp.where(live[:, :, None], user_maps, 0.0).astype(BF16)
    tile_terms = jnp.einsum(
        "ksrt,krc->kstc", tile_values, user_maps, preferred_element_type=F32
    ).astype(BF16)
    tile_terms = tile_terms.reshape(slot_count, tile_width * rank_size)
    row_count = tiles_owned * tile_width * user_count
    wanted = jnp.arange(row_count // tile_width, dtype=jnp.int32)
    hits = (flat_ids[None, :] == wanted[:, None]).astype(BF16)
    summed = jnp.dot(hits, tile_terms, preferred_element_type=F32)
    item_mttkrp = lax.psum_scatter(
        summed.reshape(row_count, rank_size).astype(BF16), "user", scatter_dimension=0, tiled=True
    ).astype(F32)
    new_items = jnp.dot(item_mttkrp, gram_inv, precision=HIGHEST)
    return (slices, new_time, new_items)


def solution(mesh):
    in_specs = (
        P("user", "item", None, None),
        P("user", "item"),
        P("user"),
        P("user", None),
        P(),
        P(("item", "user"), None),
    )
    out_specs = (P(("user", "item"), None, None), P(), P(("item", "user"), None))
    return jax.shard_map(body, mesh=mesh, in_specs=in_specs, out_specs=out_specs, check_vma=False)
```

```python
import functools

import jax
import jax.numpy as jnp
from jax import lax
from jax.experimental import pallas as pl
from jax.experimental.pallas import tpu as pltpu
from jax.sharding import PartitionSpec as P

NS_STEPS = 6
HIGHEST = lax.Precision.HIGHEST
EPSILON = 1e-06
F32, BF16 = jnp.float32, jnp.bfloat16
VMEM = pl.BlockSpec(memory_space=pltpu.VMEM)


def send(src, dst, send_sem, recv_sem, **peer):
    return pltpu.make_async_remote_copy(
        src_ref=src,
        dst_ref=dst,
        send_sem=send_sem,
        recv_sem=recv_sem,
        device_id=peer,
        device_id_type=pl.DeviceIdType.MESH,
    )


def places():
    user, item = lax.axis_index("user"), lax.axis_index("item")
    return user // 4, user % 4, item // 2, item % 2, item


def y_peer(y, z, d):
    return ((y + d) % 4) * 4 + z


def z_peer(y, z, d):
    return y * 4 + (z + d) % 4


def greet(y, z, item):
    barrier = pltpu.get_barrier_semaphore()
    for d in range(1, 8):
        pl.semaphore_signal(
            barrier, inc=1, device_id={"item": (item + d) % 8}, device_id_type=pl.DeviceIdType.MESH
        )
    for d in range(1, 4):
        for peer in (y_peer(y, z, d), z_peer(y, z, d)):
            pl.semaphore_signal(
                barrier, inc=1, device_id={"user": peer}, device_id_type=pl.DeviceIdType.MESH
            )
    pl.semaphore_wait(barrier, 13)


def split(a):
    high = a.astype(BF16)
    return high, (a - high.astype(F32)).astype(BF16)


def dot3(a, b, dims):
    contract = ((dims[0],), (dims[1],)), ((), ())
    one = functools.partial(lax.dot_general, dimension_numbers=contract, preferred_element_type=F32)
    return one(a[0], b[0]) + (one(a[0], b[1]) + one(a[1], b[0]))


def rows_of(j):
    return pl.ds(pl.multiple_of(j * 32, 32), 32)


def scatter_start(term, buf, sems, base, item):
    copies = []
    for d in range(1, 8):
        j = (item + d) % 8
        copies.append(
            send(term.at[rows_of(j)], buf.at[item], sems[0].at[base + d], sems[1].at[base + d], item=j)
        )
        copies[-1].start()
    buf[item] = term[rows_of(item)]
    return copies


def share_start(buf, sems, base, at, peer_of, value):
    buf[at] = value
    copies = []
    for d in range(1, 4):
        copies.append(
            send(buf.at[at], buf.at[at], sems[0].at[base + d], sems[1].at[base + d], user=peer_of(d))
        )
        copies[-1].start()
    return copies


def gather_start(full, sems, base, item, value):
    full[rows_of(item)] = value
    copies = []
    for d in range(1, 8):
        part = full.at[rows_of(item)]
        copies.append(
            send(part, part, sems[0].at[base + d], sems[1].at[base + d], item=(item + d) % 8)
        )
        copies[-1].start()
    return copies


def arrive(copies):
    for copy in copies:
        copy.wait_recv()


def total_of(buf, count):
    total = buf[0]
    for n in range(1, count):
        total = total + buf[n]
    return total


def sum_kernel(
    term, weights, lists, full, all_weights, lists_y, lists_z, buf_x, buf_y, buf_z, send_sem, recv_sem
):
    sems = (send_sem, recv_sem)
    y, z, _, _, item = places()
    all_weights[y, z] = weights[...]
    lists_y[y] = lists[...]
    lists_z[z] = lists[...]
    greet(y, z, item)
    started = scatter_start(term, buf_x, sems, 0, item)
    names = []
    for d in range(1, 4):
        for n, held, at, peer in (
            (32, lists_y, y, y_peer(y, z, d)),
            (36, lists_z, z, z_peer(y, z, d)),
        ):
            names.append(
                send(lists, held.at[at], send_sem.at[n + d], recv_sem.at[n + d], user=peer)
            )
            names[-1].start()
    wide = []
    for d in range(1, 4):
        mine = all_weights.at[y, z]
        wide.append(
            send(mine, mine, send_sem.at[24 + d], recv_sem.at[24 + d], user=y_peer(y, z, d))
        )
        wide[-1].start()
    arrive(started)
    step = share_start(
        buf_y, sems, 8, y, functools.partial(y_peer, y, z), total_of(buf_x, 8)
    )
    arrive(wide)
    for d in range(1, 4):
        mine = all_weights.at[:, z]
        wide.append(
            send(mine, mine, send_sem.at[28 + d], recv_sem.at[28 + d], user=z_peer(y, z, d))
        )
        wide[-1].start()
    arrive(step)
    started += step
    step = share_start(
        buf_z, sems, 12, z, functools.partial(z_peer, y, z), total_of(buf_y, 4)
    )
    arrive(step)
    started += step
    step = gather_start(full, sems, 16, item, total_of(buf_z, 4))
    arrive(step)
    arrive(wide[3:])
    arrive(names)
    for copy in started + step + wide + names:
        copy.wait_send()


def sum_everywhere(term, weights, lists):
    return pl.pallas_call(
        sum_kernel,
        out_shape=(
            jax.ShapeDtypeStruct((256, 256), F32),
            jax.ShapeDtypeStruct((4, 4, 16, 256), F32),
            jax.ShapeDtypeStruct((4, 8, 128), jnp.int32),
            jax.ShapeDtypeStruct((4, 8, 128), jnp.int32),
        ),
        in_specs=[VMEM] * 3,
        out_specs=(VMEM,) * 4,
        scratch_shapes=[
            pltpu.VMEM((8, 32, 256), F32),
            pltpu.VMEM((4, 32, 256), F32),
            pltpu.VMEM((4, 32, 256), F32),
            pltpu.SemaphoreType.DMA((40,)),
            pltpu.SemaphoreType.DMA((40,)),
        ],
        compiler_params=pltpu.CompilerParams(collective_id=0, has_side_effects=True),
        name="sum_everywhere",
    )(term, weights, lists)


def mid_kernel(
    partial,
    weights,
    time_factor,
    inner_inv,
    weight_gram,
    polar_all,
    slices,
    new_time,
    item_gram,
    recv1,
    outgoing,
    relay,
    recv2,
    scaled,
    iterate,
    term,
    full,
    buf_x,
    buf_y,
    buf_z,
    send_sem,
    recv_sem,
):
    sems = (send_sem, recv_sem)
    y, z, x, core, item = places()
    partner = x * 2 + (1 - core)
    right, left = ((x + 1) % 4) * 2 + core, ((x + 3) % 4) * 2 + core
    done = []

    def go(src, dst, n, **peer):
        copy = send(src, dst, send_sem.at[n], recv_sem.at[n], **peer)
        copy.start()
        done.append(copy)
        return copy

    greet(y, z, item)

    def share(d):
        return (((x + d) % 4) * 2 + core) * 2

    def other_share(d):
        return (((x + d) % 4) * 2 + (1 - core)) * 2

    cross = {}
    for d in (2, 1, 3, 0):
        cross[d] = go(partial.at[pl.ds(other_share(d), 2)], recv1.at[d], d, item=partner)
    cross[2].wait_recv()
    outgoing[0] = (partial[share(2)] + recv1[2, 0]).astype(BF16)
    far_right = go(outgoing.at[0], relay.at[0], 4, item=right)
    outgoing[1] = (partial[share(2) + 1] + recv1[2, 1]).astype(BF16)
    far_left = go(outgoing.at[1], relay.at[1], 5, item=left)
    cross[1].wait_recv()
    outgoing[3] = (partial[share(1) + 1] + recv1[1, 1]).astype(BF16)
    near_right = go(outgoing.at[3], recv2.at[0], 6, item=right)
    cross[3].wait_recv()
    outgoing[4] = (partial[share(3)] + recv1[3, 0]).astype(BF16)
    near_left = go(outgoing.at[4], recv2.at[1], 7, item=left)
    far_right.wait_recv()
    outgoing[2] = (partial[share(1)] + recv1[1, 0] + relay[0].astype(F32)).astype(BF16)
    sum_right = go(outgoing.at[2], recv2.at[2], 8, item=right)
    far_left.wait_recv()
    outgoing[5] = (partial[share(3) + 1] + recv1[3, 1] + relay[1].astype(F32)).astype(BF16)
    sum_left = go(outgoing.at[5], recv2.at[3], 9, item=left)
    cross[0].wait_recv()
    for copy in (near_right, near_left, sum_right, sum_left):
        copy.wait_recv()
    factor = split(time_factor[...])
    for k, parts in enumerate(((2, 1), (0, 3))):
        projection = partial[share(0) + k] + recv1[0, k]
        for n in parts:
            projection = projection + recv2[n].astype(F32)
        projection = projection * weights[k]
        scaled[k] = projection
        target = dot3(split(projection), factor, (1, 1))
        norm = jnp.sum(target * target, axis=(0, 1), keepdims=True) + EPSILON
        iterate[k] = target / jnp.sqrt(norm)

    def sweep(_, carry):
        for k in range(2):
            now = iterate[k]
            parts = split(now)
            gram = dot3(parts, parts, (1, 1))
            iterate[k] = 1.5 * now - 0.5 * dot3(split(gram), parts, (1, 0))
        return carry

    lax.fori_loop(0, NS_STEPS, sweep, 0)
    total = None
    for k in range(2):
        polar = iterate[k]
        slices[k] = polar.astype(BF16)
        polar_all[item * 2 + k] = polar.astype(BF16)
        one = dot3(split(polar.T), split(scaled[k]), (1, 0))
        total = one if total is None else total + one
    term[...] = total
    step = scatter_start(term, buf_x, sems, 16, item)
    done.extend(step)
    mine = polar_all.at[pl.ds(item * 2, 2)]
    own_right = go(mine, mine, 48, item=right)
    own_left = go(mine, mine, 49, item=left)
    crossing = [go(mine, mine, 50, item=partner)]
    arrive(step)
    step = share_start(buf_y, sems, 24, y, functools.partial(y_peer, y, z), total_of(buf_x, 8))
    done.extend(step)
    arrive(step)
    step = share_start(buf_z, sems, 28, z, functools.partial(z_peer, y, z), total_of(buf_y, 4))
    done.extend(step)
    own_right.wait_recv()
    hop = polar_all.at[left * 2]
    hop_right = go(hop, hop, 51, item=right)
    own_left.wait_recv()
    hop = polar_all.at[right * 2 + 1]
    hop_left = go(hop, hop, 52, item=left)
    for n, source in ((53, left), (54, right)):
        block = polar_all.at[pl.ds(source * 2, 2)]
        crossing.append(go(block, block, n, item=partner))
    arrive(step)
    step = gather_start(full, sems, 32, item, total_of(buf_z, 4))
    done.extend(step)
    hop_right.wait_recv()
    hop_left.wait_recv()
    block = polar_all.at[pl.ds(share(2), 2)]
    crossing.append(go(block, block, 55, item=partner))
    arrive(step)
    raw = dot3(split(full[...]), split(inner_inv[...]), (1, 0))
    fresh = raw / jnp.sqrt(jnp.sum(raw * raw, axis=0, keepdims=True) + EPSILON)
    new_time[...] = fresh
    item_gram[...] = dot3(split(fresh.T), split(fresh), (1, 0)) * weight_gram[...]
    arrive(crossing)
    for copy in done:
        copy.wait_send()


def middle(partial, weights, time_factor, inner_inv, weight_gram):
    return pl.pallas_call(
        mid_kernel,
        out_shape=(
            jax.ShapeDtypeStruct((16, 256, 256), BF16),
            jax.ShapeDtypeStruct((2, 256, 256), BF16),
            jax.ShapeDtypeStruct((256, 256), F32),
            jax.ShapeDtypeStruct((256, 256), F32),
        ),
        in_specs=[VMEM] * 5,
        out_specs=(VMEM,) * 4,
        scratch_shapes=[
            pltpu.VMEM((4, 2, 256, 256), F32),
            pltpu.VMEM((6, 256, 256), BF16),
            pltpu.VMEM((2, 256, 256), BF16),
            pltpu.VMEM((4, 256, 256), BF16),
            pltpu.VMEM((2, 256, 256), F32),
            pltpu.VMEM((2, 256, 256), F32),
            pltpu.VMEM((256, 256), F32),
            pltpu.VMEM((256, 256), F32),
            pltpu.VMEM((8, 32, 256), F32),
            pltpu.VMEM((4, 32, 256), F32),
            pltpu.VMEM((4, 32, 256), F32),
            pltpu.SemaphoreType.DMA((56,)),
            pltpu.SemaphoreType.DMA((56,)),
        ],
        compiler_params=pltpu.CompilerParams(collective_id=1, has_side_effects=True),
        name="middle",
    )(partial, weights, time_factor, inner_inv, weight_gram)


def invert_half(matrix):
    down = lax.broadcasted_iota(jnp.int32, (128, 128), 0)
    across = lax.broadcasted_iota(jnp.int32, (128, 128), 1)
    lanes = lax.broadcasted_iota(jnp.int32, (1, 128), 1)
    subs = lax.broadcasted_iota(jnp.int32, (128, 1), 0)

    def step(t, a):
        k0, k1 = 2 * t, 2 * t + 1
        r0 = jnp.sum(jnp.where(down == k0, a, 0.0), axis=0, keepdims=True)
        r1 = jnp.sum(jnp.where(down == k1, a, 0.0), axis=0, keepdims=True)
        c0 = jnp.sum(jnp.where(across == k0, a, 0.0), axis=1, keepdims=True)
        c1 = jnp.sum(jnp.where(across == k1, a, 0.0), axis=1, keepdims=True)
        p00 = jnp.sum(jnp.where(lanes == k0, r0, 0.0), axis=1, keepdims=True)
        p01 = jnp.sum(jnp.where(lanes == k1, r0, 0.0), axis=1, keepdims=True)
        p10 = jnp.sum(jnp.where(lanes == k0, r1, 0.0), axis=1, keepdims=True)
        p11 = jnp.sum(jnp.where(lanes == k1, r1, 0.0), axis=1, keepdims=True)
        i0 = 1.0 / p00
        g, h = p01 * i0, p10 * i0
        q11 = 1.0 / (p11 - p10 * g)
        q01, q10 = -g * q11, -h * q11
        q00 = i0 - g * q10
        r0 = jnp.where(lanes == k0, 1.0, jnp.where(lanes == k1, 0.0, r0))
        r1 = jnp.where(lanes == k1, 1.0, jnp.where(lanes == k0, 0.0, r1))
        c0 = jnp.where(subs == k0, -1.0, jnp.where(subs == k1, 0.0, c0))
        c1 = jnp.where(subs == k1, -1.0, jnp.where(subs == k0, 0.0, c1))
        u0, u1 = c0 * q00 + c1 * q10, c0 * q01 + c1 * q11
        gone = (down == k0) | (down == k1) | (across == k0) | (across == k1)
        return jnp.where(gone, 0.0, a) - u0 * r0 - u1 * r1

    return lax.fori_loop(0, 64, step, matrix)


def full_dot(a, b):
    return jnp.dot(a, b, precision=HIGHEST, preferred_element_type=F32)


LOW, HIGH = pl.ds(0, 128), pl.ds(128, 128)


def invert_first(gram, out, work):
    first = invert_half(gram[LOW, LOW])
    out[LOW, LOW] = first
    work[0] = full_dot(first, gram[LOW, HIGH])
    work[1] = gram[HIGH, HIGH] - full_dot(gram[HIGH, LOW], work[0])


def invert_second(out, work):
    second = invert_half(work[1])
    out[HIGH, HIGH] = second
    cross = full_dot(work[0], second)
    out[LOW, HIGH] = -cross
    out[HIGH, LOW] = -cross.T
    out[LOW, LOW] = out[LOW, LOW] + full_dot(cross, work[0].T)


def greet_plane(y, z):
    barrier = pltpu.get_barrier_semaphore()
    for d in (1, 3):
        for peer in (y_peer(y, z, d), z_peer(y, z, d)):
            pl.semaphore_signal(
                barrier, inc=1, device_id={"user": peer}, device_id_type=pl.DeviceIdType.MESH
            )
    pl.semaphore_wait(barrier, 4)


def terms_kernel(
    polar_all,
    new_time,
    weight_cols,
    values,
    item_gram,
    lengths,
    slot_of,
    lists_y,
    lists_z,
    summed,
    gram_inv,
    terms,
    slots,
    got,
    via,
    hold,
    out2,
    via2,
    fin,
    work,
    send_sem,
    recv_sem,
):
    y, z, _, _, _ = places()
    done = []

    def go(src, dst, n, peer):
        copy = send(src, dst, send_sem.at[n], recv_sem.at[n], user=peer)
        copy.start()
        done.append(copy)
        return copy

    first, second = (z, y), (y, z)
    first_peer = (functools.partial(z_peer, y, z), functools.partial(y_peer, y, z))
    second_peer = (functools.partial(y_peer, y, z), functools.partial(z_peer, y, z))
    lists = (lists_z, lists_y)

    def owner(h, a, b):
        return b * 4 + a if h == 0 else a * 4 + b

    greet_plane(y, z)
    time_parts = split(new_time[...].T)
    lanes = lax.broadcasted_iota(jnp.int32, (256, 256), 1)

    def one_user(k, carry):
        dims = (((1,), (1,)), ((), ()))
        polar = polar_all[k]
        maps = lax.dot_general(time_parts[0], polar, dims, preferred_element_type=F32)
        maps = maps + lax.dot_general(time_parts[1], polar, dims, preferred_element_type=F32)
        maps = jnp.where(lanes < lengths[k], maps * weight_cols[k], 0.0).astype(BF16)
        for s in range(4):
            terms[4 * k + s] = jnp.dot(
                maps, values[4 * k + s], preferred_element_type=F32
            ).astype(BF16)
        return carry

    lax.fori_loop(0, 16, one_user, 0)

    def pack(h, d):
        a = (first[h] + d) % 4

        def one(q, carry):
            place = owner(h, a, q // 8) * 8 + q % 8
            slots[h, a, q] = terms[slot_of[place], pl.ds(h * 128, 128), :]
            return carry

        lax.fori_loop(0, 32, one, 0, unroll=4)
        return a

    far = {}
    for h in range(2):
        a = pack(h, 2)
        far[h, 1] = go(
            slots.at[h, a, pl.ds(0, 16)], via.at[h, 0], 12 * h, first_peer[h](1)
        )
        far[h, 3] = go(
            slots.at[h, a, pl.ds(16, 16)], via.at[h, 1], 12 * h + 1, first_peer[h](3)
        )
    near = []
    for h in range(2):
        for d in (1, 3):
            a = pack(h, d)
            near.append(
                go(slots.at[h, a], got.at[h, first[h]], 12 * h + 1 + d, first_peer[h](d))
            )
    for h in range(2):
        pack(h, 0)
    invert_first(item_gram, gram_inv, work)
    for h in range(2):
        far[h, 1].wait_recv()
        far[h, 3].wait_recv()
        before, after = (first[h] + 3) % 4, (first[h] + 1) % 4
        near.append(
            go(via.at[h, 0], got.at[h, before, pl.ds(0, 16)], 12 * h + 3, first_peer[h](1))
        )
        near.append(
            go(via.at[h, 1], got.at[h, after, pl.ds(16, 16)], 12 * h + 5, first_peer[h](3))
        )
    invert_second(gram_inv, work)
    arrive(near)

    def dense(h, d, start, store):
        b = (second[h] + d) % 4
        place = owner(h, first[h], b) * 16

        def one(n, carry):
            tile = place + start + n
            total = None
            for e in range(4):
                source = (first[h] + e) % 4
                rank = lists[h][source, 1 + tile // 128, tile % 128]
                slot = b * 8 + jnp.maximum(rank, 0)
                block = slots[h, first[h], slot] if e == 0 else got[h, source, slot]
                block = jnp.where(rank >= 0, block.astype(F32), 0.0)
                total = block if total is None else total + block
            store(n, total)
            return carry

        lax.fori_loop(0, 8, one, 0)

    def into_out(h, part):
        def store(n, total):
            out2[h, part, n] = total.astype(BF16)

        return store

    def into_hold(h, part):
        def store(n, total):
            hold[h, part, n] = total

        return store

    def into_sum(h, start):
        def store(n, total):
            summed[start + n, pl.ds(h * 128, 128), :] = total

        return store

    far2 = {}
    for h in range(2):
        for part, start, d in ((0, 0, 1), (1, 8, 3)):
            dense(h, 2, start, into_out(h, part))
            far2[h, d] = go(
                out2.at[h, part], via2.at[h, part], 12 * h + 6 + part, second_peer[h](d)
            )
    last = []
    for h in range(2):
        for part, start, d in ((2, 8, 1), (3, 0, 3)):
            dense(h, d, start, into_out(h, part))
            last.append(
                go(out2.at[h, part], fin.at[h, part - 2], 12 * h + 6 + part, second_peer[h](d))
            )
    for h in range(2):
        dense(h, 1, 0, into_hold(h, 0))
        dense(h, 3, 8, into_hold(h, 1))
    for h in range(2):
        for part, d in ((0, 1), (1, 3)):
            far2[h, d].wait_recv()

            def merge(n, carry, h=h, part=part):
                both = hold[h, part, n] + via2[h, part, n].astype(F32)
                out2[h, 4 + part, n] = both.astype(BF16)
                return carry

            lax.fori_loop(0, 8, merge, 0)
            last.append(
                go(
                    out2.at[h, 4 + part],
                    fin.at[h, 2 + part],
                    12 * h + 10 + part,
                    second_peer[h](d),
                )
            )
    for h in range(2):
        dense(h, 0, 0, into_sum(h, 0))
        dense(h, 0, 8, into_sum(h, 8))
    arrive(last)
    for h in range(2):
        for start, parts in ((0, (1, 2)), (8, (0, 3))):

            def close(n, carry, h=h, start=start, parts=parts):
                total = summed[start + n, pl.ds(h * 128, 128), :]
                for part in parts:
                    total = total + fin[h, part, n].astype(F32)
                summed[start + n, pl.ds(h * 128, 128), :] = total
                return carry

            lax.fori_loop(0, 8, close, 0)
    for copy in done:
        copy.wait_send()


def sum_terms(
    polar_all, new_time, weight_cols, values, item_gram, lengths, slot_of, lists_y, lists_z
):
    smem = pl.BlockSpec(memory_space=pltpu.SMEM)
    block = (128, 128)
    return pl.pallas_call(
        terms_kernel,
        out_shape=(
            jax.ShapeDtypeStruct((16, 256, 128), F32),
            jax.ShapeDtypeStruct((256, 256), F32),
        ),
        in_specs=[VMEM] * 5 + [smem] * 4,
        out_specs=(VMEM,) * 2,
        scratch_shapes=[
            pltpu.VMEM((64, 256, 128), BF16),
            pltpu.VMEM((2, 4, 32) + block, BF16),
            pltpu.VMEM((2, 4, 32) + block, BF16),
            pltpu.VMEM((2, 2, 16) + block, BF16),
            pltpu.VMEM((2, 2, 8) + block, F32),
            pltpu.VMEM((2, 6, 8) + block, BF16),
            pltpu.VMEM((2, 2, 8) + block, BF16),
            pltpu.VMEM((2, 4, 8) + block, BF16),
            pltpu.VMEM((2,) + block, F32),
            pltpu.SemaphoreType.DMA((24,)),
            pltpu.SemaphoreType.DMA((24,)),
        ],
        compiler_params=pltpu.CompilerParams(collective_id=2, has_side_effects=True),
        name="sum_terms",
    )(polar_all, new_time, weight_cols, values, item_gram, lengths, slot_of, lists_y, lists_z)


def tile_tables(tiles):
    count = tiles.shape[0]
    owners, inside = tiles // 16, tiles % 16
    order = jnp.arange(count, dtype=jnp.int32)
    same = (owners[:, None] == owners[None, :]) & (order[None, :] < order[:, None])
    rank = jnp.sum(same.astype(jnp.int32), axis=1)
    place = owners * 8 + rank
    hit = place[None, :] == jnp.arange(128, dtype=jnp.int32)[:, None]
    want = jnp.sum(jnp.where(hit, inside[None, :], 0), axis=1)
    slot_of = jnp.sum(jnp.where(hit, order[None, :], 0), axis=1)
    named = tiles[None, :] == jnp.arange(256, dtype=jnp.int32)[:, None]
    rank_of = jnp.sum(jnp.where(named, rank[None, :] + 1, 0), axis=1) - 1
    lists = jnp.concatenate([want, rank_of, jnp.zeros((640,), jnp.int32)]).reshape(8, 128)
    return place, slot_of, lists


def spd_inverse(gram):
    lower = jnp.linalg.cholesky(gram)
    return jax.scipy.linalg.cho_solve((lower, True), jnp.eye(gram.shape[0], dtype=F32))


def body(tile_values, tile_ids, lengths, user_weights, time_factor, item_factor):
    user_count = lax.axis_size("user")
    item_count = lax.axis_size("item")
    item_pos = lax.axis_index("item")
    users_here, slots_user, time_rows, tile_width = tile_values.shape
    rank_size = time_factor.shape[0]
    tiles_owned = item_factor.shape[0] // tile_width
    slot_count = users_here * slots_user
    share_count = users_here // item_count
    flat_ids = (tile_ids - item_pos * (tiles_owned * user_count)).reshape(slot_count)
    live = jnp.arange(time_rows, dtype=jnp.int32)[None, :] < lengths[:, None]
    shard_rows = lax.all_gather(item_factor, "user", axis=0, tiled=True)
    item_term = lax.dot_general(
        item_factor, item_factor, (((0,), (0,)), ((), ())), preferred_element_type=F32
    )
    _, slot_of, lists = tile_tables(flat_ids)
    item_inner, all_weights, lists_y, lists_z = sum_everywhere(item_term, user_weights, lists)
    all_weights = all_weights.reshape(user_count * users_here, rank_size)
    weight_gram = jnp.dot(all_weights.T, all_weights, precision=HIGHEST)
    inner_inv = spd_inverse(item_inner * weight_gram)
    panels = shard_rows.reshape(tiles_owned * user_count, tile_width, rank_size)[flat_ids]
    panels = panels.reshape(users_here, slots_user, tile_width, rank_size)
    partial = jnp.einsum("ksrt,kstc->krc", tile_values, panels, preferred_element_type=F32)
    partial = jnp.where(live[:, :, None], partial, 0.0)
    share_weights = lax.dynamic_slice_in_dim(user_weights, item_pos * share_count, share_count, 0)
    polar_all, slices, new_time, item_gram = middle(
        partial, share_weights[:, None, :], time_factor, inner_inv, weight_gram
    )
    values = tile_values.reshape(slot_count, time_rows, tile_width)
    summed, gram_inv = sum_terms(
        polar_all,
        new_time,
        user_weights[:, :, None],
        values,
        item_gram,
        lengths,
        slot_of,
        lists_y,
        lists_z,
    )
    new_items = jnp.einsum("nct,cd->ntd", summed, gram_inv, precision=HIGHEST)
    new_items = new_items.reshape(item_factor.shape)
    return (slices, new_time, new_items)


def solution(mesh):
    in_specs = (
        P("user", "item", None, None),
        P("user", "item"),
        P("user"),
        P("user", None),
        P(),
        P(("item", "user"), None),
    )
    out_specs = (P(("user", "item"), None, None), P(), P(("item", "user"), None))
    return jax.shard_map(body, mesh=mesh, in_specs=in_specs, out_specs=out_specs, check_vma=False)
```

```python
import functools

import jax
import jax.numpy as jnp
from jax import lax
from jax.experimental import pallas as pl
from jax.experimental.pallas import tpu as pltpu
from jax.sharding import PartitionSpec as P

NS_STEPS = 6
HIGHEST = lax.Precision.HIGHEST
EPSILON = 1e-06
F32, BF16 = jnp.float32, jnp.bfloat16
VMEM = pl.BlockSpec(memory_space=pltpu.VMEM)


def send(src, dst, send_sem, recv_sem, **peer):
    return pltpu.make_async_remote_copy(
        src_ref=src,
        dst_ref=dst,
        send_sem=send_sem,
        recv_sem=recv_sem,
        device_id=peer,
        device_id_type=pl.DeviceIdType.MESH,
    )


def places():
    user, item = lax.axis_index("user"), lax.axis_index("item")
    return user // 4, user % 4, item // 2, item % 2, item


def y_peer(y, z, d):
    return ((y + d) % 4) * 4 + z


def z_peer(y, z, d):
    return y * 4 + (z + d) % 4


def greet(y, z, item):
    barrier = pltpu.get_barrier_semaphore()
    for d in range(1, 8):
        pl.semaphore_signal(
            barrier, inc=1, device_id={"item": (item + d) % 8}, device_id_type=pl.DeviceIdType.MESH
        )
    for d in range(1, 4):
        for peer in (y_peer(y, z, d), z_peer(y, z, d)):
            pl.semaphore_signal(
                barrier, inc=1, device_id={"user": peer}, device_id_type=pl.DeviceIdType.MESH
            )
    pl.semaphore_wait(barrier, 13)


def split(a):
    high = a.astype(BF16)
    return high, (a - high.astype(F32)).astype(BF16)


def dot3(a, b, dims):
    contract = ((dims[0],), (dims[1],)), ((), ())
    one = functools.partial(lax.dot_general, dimension_numbers=contract, preferred_element_type=F32)
    return one(a[0], b[0]) + (one(a[0], b[1]) + one(a[1], b[0]))


def rows_of(j):
    return pl.ds(pl.multiple_of(j * 32, 32), 32)


def scatter_start(term, buf, sems, base, item):
    copies = []
    for d in range(1, 8):
        j = (item + d) % 8
        copies.append(
            send(term.at[rows_of(j)], buf.at[item], sems[0].at[base + d], sems[1].at[base + d], item=j)
        )
        copies[-1].start()
    buf[item] = term[rows_of(item)]
    return copies


def share_start(buf, sems, base, at, peer_of, value):
    buf[at] = value
    copies = []
    for d in range(1, 4):
        copies.append(
            send(buf.at[at], buf.at[at], sems[0].at[base + d], sems[1].at[base + d], user=peer_of(d))
        )
        copies[-1].start()
    return copies


def gather_start(full, sems, base, item, value):
    full[rows_of(item)] = value
    copies = []
    for d in range(1, 8):
        part = full.at[rows_of(item)]
        copies.append(
            send(part, part, sems[0].at[base + d], sems[1].at[base + d], item=(item + d) % 8)
        )
        copies[-1].start()
    return copies


def arrive(copies):
    for copy in copies:
        copy.wait_recv()


def total_of(buf, count):
    total = buf[0]
    for n in range(1, count):
        total = total + buf[n]
    return total


def mid_kernel(
    partial,
    weights,
    time_factor,
    inner_inv,
    weight_gram,
    polar_all,
    slices,
    new_time,
    item_gram,
    recv1,
    outgoing,
    relay,
    recv2,
    scaled,
    iterate,
    term,
    full,
    buf_x,
    buf_y,
    buf_z,
    send_sem,
    recv_sem,
):
    sems = (send_sem, recv_sem)
    y, z, x, core, item = places()
    partner = x * 2 + (1 - core)
    right, left = ((x + 1) % 4) * 2 + core, ((x + 3) % 4) * 2 + core
    done = []

    def go(src, dst, n, **peer):
        copy = send(src, dst, send_sem.at[n], recv_sem.at[n], **peer)
        copy.start()
        done.append(copy)
        return copy

    greet(y, z, item)

    def share(d):
        return (((x + d) % 4) * 2 + core) * 2

    def other_share(d):
        return (((x + d) % 4) * 2 + (1 - core)) * 2

    cross = {}
    for d in (2, 1, 3, 0):
        cross[d] = go(partial.at[pl.ds(other_share(d), 2)], recv1.at[d], d, item=partner)
    cross[2].wait_recv()
    outgoing[0] = (partial[share(2)] + recv1[2, 0]).astype(BF16)
    far_right = go(outgoing.at[0], relay.at[0], 4, item=right)
    outgoing[1] = (partial[share(2) + 1] + recv1[2, 1]).astype(BF16)
    far_left = go(outgoing.at[1], relay.at[1], 5, item=left)
    cross[1].wait_recv()
    outgoing[3] = (partial[share(1) + 1] + recv1[1, 1]).astype(BF16)
    near_right = go(outgoing.at[3], recv2.at[0], 6, item=right)
    cross[3].wait_recv()
    outgoing[4] = (partial[share(3)] + recv1[3, 0]).astype(BF16)
    near_left = go(outgoing.at[4], recv2.at[1], 7, item=left)
    far_right.wait_recv()
    outgoing[2] = (partial[share(1)] + recv1[1, 0] + relay[0].astype(F32)).astype(BF16)
    sum_right = go(outgoing.at[2], recv2.at[2], 8, item=right)
    far_left.wait_recv()
    outgoing[5] = (partial[share(3) + 1] + recv1[3, 1] + relay[1].astype(F32)).astype(BF16)
    sum_left = go(outgoing.at[5], recv2.at[3], 9, item=left)
    cross[0].wait_recv()
    for copy in (near_right, near_left, sum_right, sum_left):
        copy.wait_recv()
    factor = split(time_factor[...])
    for k, parts in enumerate(((2, 1), (0, 3))):
        projection = partial[share(0) + k] + recv1[0, k]
        for n in parts:
            projection = projection + recv2[n].astype(F32)
        projection = projection * weights[k]
        scaled[k] = projection
        target = dot3(split(projection), factor, (1, 1))
        norm = jnp.sum(target * target, axis=(0, 1), keepdims=True) + EPSILON
        iterate[k] = target / jnp.sqrt(norm)

    def sweep(_, carry):
        for k in range(2):
            now = iterate[k]
            parts = split(now)
            gram = dot3(parts, parts, (1, 1))
            iterate[k] = 1.5 * now - 0.5 * dot3(split(gram), parts, (1, 0))
        return carry

    lax.fori_loop(0, NS_STEPS, sweep, 0)
    total = None
    for k in range(2):
        polar = iterate[k]
        slices[k] = polar.astype(BF16)
        polar_all[item * 2 + k] = polar.astype(BF16)
        one = dot3(split(polar.T), split(scaled[k]), (1, 0))
        total = one if total is None else total + one
    term[...] = total
    step = scatter_start(term, buf_x, sems, 16, item)
    done.extend(step)
    mine = polar_all.at[pl.ds(item * 2, 2)]
    own_right = go(mine, mine, 48, item=right)
    own_left = go(mine, mine, 49, item=left)
    crossing = [go(mine, mine, 50, item=partner)]
    arrive(step)
    step = share_start(buf_y, sems, 24, y, functools.partial(y_peer, y, z), total_of(buf_x, 8))
    done.extend(step)
    arrive(step)
    step = share_start(buf_z, sems, 28, z, functools.partial(z_peer, y, z), total_of(buf_y, 4))
    done.extend(step)
    own_right.wait_recv()
    hop = polar_all.at[left * 2]
    hop_right = go(hop, hop, 51, item=right)
    own_left.wait_recv()
    hop = polar_all.at[right * 2 + 1]
    hop_left = go(hop, hop, 52, item=left)
    for n, source in ((53, left), (54, right)):
        block = polar_all.at[pl.ds(source * 2, 2)]
        crossing.append(go(block, block, n, item=partner))
    arrive(step)
    step = gather_start(full, sems, 32, item, total_of(buf_z, 4))
    done.extend(step)
    hop_right.wait_recv()
    hop_left.wait_recv()
    block = polar_all.at[pl.ds(share(2), 2)]
    crossing.append(go(block, block, 55, item=partner))
    arrive(step)
    raw = dot3(split(full[...]), split(inner_inv[...]), (1, 0))
    fresh = raw / jnp.sqrt(jnp.sum(raw * raw, axis=0, keepdims=True) + EPSILON)
    new_time[...] = fresh
    item_gram[...] = dot3(split(fresh.T), split(fresh), (1, 0)) * weight_gram[...]
    arrive(crossing)
    for copy in done:
        copy.wait_send()


def middle(partial, weights, time_factor, inner_inv, weight_gram):
    return pl.pallas_call(
        mid_kernel,
        out_shape=(
            jax.ShapeDtypeStruct((16, 256, 256), BF16),
            jax.ShapeDtypeStruct((2, 256, 256), BF16),
            jax.ShapeDtypeStruct((256, 256), F32),
            jax.ShapeDtypeStruct((256, 256), F32),
        ),
        in_specs=[VMEM] * 5,
        out_specs=(VMEM,) * 4,
        scratch_shapes=[
            pltpu.VMEM((4, 2, 256, 256), F32),
            pltpu.VMEM((6, 256, 256), BF16),
            pltpu.VMEM((2, 256, 256), BF16),
            pltpu.VMEM((4, 256, 256), BF16),
            pltpu.VMEM((2, 256, 256), F32),
            pltpu.VMEM((2, 256, 256), F32),
            pltpu.VMEM((256, 256), F32),
            pltpu.VMEM((256, 256), F32),
            pltpu.VMEM((8, 32, 256), F32),
            pltpu.VMEM((4, 32, 256), F32),
            pltpu.VMEM((4, 32, 256), F32),
            pltpu.SemaphoreType.DMA((56,)),
            pltpu.SemaphoreType.DMA((56,)),
        ],
        compiler_params=pltpu.CompilerParams(collective_id=1, has_side_effects=True),
        name="middle",
    )(partial, weights, time_factor, inner_inv, weight_gram)


def invert_half(matrix):
    down = lax.broadcasted_iota(jnp.int32, (128, 128), 0)
    across = lax.broadcasted_iota(jnp.int32, (128, 128), 1)
    lanes = lax.broadcasted_iota(jnp.int32, (1, 128), 1)
    subs = lax.broadcasted_iota(jnp.int32, (128, 1), 0)

    def step(t, a):
        k0, k1 = 2 * t, 2 * t + 1
        r0 = jnp.sum(jnp.where(down == k0, a, 0.0), axis=0, keepdims=True)
        r1 = jnp.sum(jnp.where(down == k1, a, 0.0), axis=0, keepdims=True)
        c0 = jnp.sum(jnp.where(across == k0, a, 0.0), axis=1, keepdims=True)
        c1 = jnp.sum(jnp.where(across == k1, a, 0.0), axis=1, keepdims=True)
        p00 = jnp.sum(jnp.where(lanes == k0, r0, 0.0), axis=1, keepdims=True)
        p01 = jnp.sum(jnp.where(lanes == k1, r0, 0.0), axis=1, keepdims=True)
        p10 = jnp.sum(jnp.where(lanes == k0, r1, 0.0), axis=1, keepdims=True)
        p11 = jnp.sum(jnp.where(lanes == k1, r1, 0.0), axis=1, keepdims=True)
        i0 = 1.0 / p00
        g, h = p01 * i0, p10 * i0
        q11 = 1.0 / (p11 - p10 * g)
        q01, q10 = -g * q11, -h * q11
        q00 = i0 - g * q10
        r0 = jnp.where(lanes == k0, 1.0, jnp.where(lanes == k1, 0.0, r0))
        r1 = jnp.where(lanes == k1, 1.0, jnp.where(lanes == k0, 0.0, r1))
        c0 = jnp.where(subs == k0, -1.0, jnp.where(subs == k1, 0.0, c0))
        c1 = jnp.where(subs == k1, -1.0, jnp.where(subs == k0, 0.0, c1))
        u0, u1 = c0 * q00 + c1 * q10, c0 * q01 + c1 * q11
        gone = (down == k0) | (down == k1) | (across == k0) | (across == k1)
        return jnp.where(gone, 0.0, a) - u0 * r0 - u1 * r1

    return lax.fori_loop(0, 64, step, matrix)


def full_dot(a, b):
    return jnp.dot(a, b, precision=HIGHEST, preferred_element_type=F32)


LOW, HIGH = pl.ds(0, 128), pl.ds(128, 128)


def invert_first(gram, out, work):
    first = invert_half(gram[LOW, LOW])
    out[LOW, LOW] = first
    work[0] = full_dot(first, gram[LOW, HIGH])
    work[1] = gram[HIGH, HIGH] - full_dot(gram[HIGH, LOW], work[0])


def invert_second(out, work):
    second = invert_half(work[1])
    out[HIGH, HIGH] = second
    cross = full_dot(work[0], second)
    out[LOW, HIGH] = -cross
    out[HIGH, LOW] = -cross.T
    out[LOW, LOW] = out[LOW, LOW] + full_dot(cross, work[0].T)


def greet_plane(y, z):
    barrier = pltpu.get_barrier_semaphore()
    for d in (1, 3):
        for peer in (y_peer(y, z, d), z_peer(y, z, d)):
            pl.semaphore_signal(
                barrier, inc=1, device_id={"user": peer}, device_id_type=pl.DeviceIdType.MESH
            )
    pl.semaphore_wait(barrier, 4)


def terms_kernel(
    polar_all,
    new_time,
    weight_cols,
    values,
    item_gram,
    lengths,
    slot_of,
    lists_y,
    lists_z,
    summed,
    gram_inv,
    terms,
    slots,
    got,
    via,
    hold,
    out2,
    via2,
    fin,
    work,
    send_sem,
    recv_sem,
):
    y, z, _, _, _ = places()
    done = []

    def go(src, dst, n, peer):
        copy = send(src, dst, send_sem.at[n], recv_sem.at[n], user=peer)
        copy.start()
        done.append(copy)
        return copy

    first, second = (z, y), (y, z)
    first_peer = (functools.partial(z_peer, y, z), functools.partial(y_peer, y, z))
    second_peer = (functools.partial(y_peer, y, z), functools.partial(z_peer, y, z))
    lists = (lists_z, lists_y)

    def owner(h, a, b):
        return b * 4 + a if h == 0 else a * 4 + b

    greet_plane(y, z)
    time_parts = split(new_time[...].T)
    lanes = lax.broadcasted_iota(jnp.int32, (256, 256), 1)

    def one_user(k, carry):
        dims = (((1,), (1,)), ((), ()))
        polar = polar_all[k]
        maps = lax.dot_general(time_parts[0], polar, dims, preferred_element_type=F32)
        maps = maps + lax.dot_general(time_parts[1], polar, dims, preferred_element_type=F32)
        maps = jnp.where(lanes < lengths[k], maps * weight_cols[k], 0.0).astype(BF16)
        for s in range(4):
            terms[4 * k + s] = jnp.dot(
                maps, values[4 * k + s], preferred_element_type=F32
            ).astype(BF16)
        return carry

    lax.fori_loop(0, 16, one_user, 0)

    def pack(h, d):
        a = (first[h] + d) % 4

        def one(q, carry):
            place = owner(h, a, q // 8) * 8 + q % 8
            slots[h, a, q] = terms[slot_of[place], pl.ds(h * 128, 128), :]
            return carry

        lax.fori_loop(0, 32, one, 0, unroll=4)
        return a

    far = {}
    for h in range(2):
        a = pack(h, 2)
        far[h, 1] = go(
            slots.at[h, a, pl.ds(0, 16)], via.at[h, 0], 12 * h, first_peer[h](1)
        )
        far[h, 3] = go(
            slots.at[h, a, pl.ds(16, 16)], via.at[h, 1], 12 * h + 1, first_peer[h](3)
        )
    near = []
    for h in range(2):
        for d in (1, 3):
            a = pack(h, d)
            near.append(
                go(slots.at[h, a], got.at[h, first[h]], 12 * h + 1 + d, first_peer[h](d))
            )
    for h in range(2):
        pack(h, 0)
    invert_first(item_gram, gram_inv, work)
    for h in range(2):
        far[h, 1].wait_recv()
        far[h, 3].wait_recv()
        before, after = (first[h] + 3) % 4, (first[h] + 1) % 4
        near.append(
            go(via.at[h, 0], got.at[h, before, pl.ds(0, 16)], 12 * h + 3, first_peer[h](1))
        )
        near.append(
            go(via.at[h, 1], got.at[h, after, pl.ds(16, 16)], 12 * h + 5, first_peer[h](3))
        )
    invert_second(gram_inv, work)
    arrive(near)

    def dense(h, d, start, store):
        b = (second[h] + d) % 4
        place = owner(h, first[h], b) * 16

        def one(n, carry):
            tile = place + start + n
            total = None
            for e in range(4):
                source = (first[h] + e) % 4
                rank = lists[h][source, 1 + tile // 128, tile % 128]
                slot = b * 8 + jnp.maximum(rank, 0)
                block = slots[h, first[h], slot] if e == 0 else got[h, source, slot]
                block = jnp.where(rank >= 0, block.astype(F32), 0.0)
                total = block if total is None else total + block
            store(n, total)
            return carry

        lax.fori_loop(0, 8, one, 0)

    def into_out(h, part):
        def store(n, total):
            out2[h, part, n] = total.astype(BF16)

        return store

    def into_hold(h, part):
        def store(n, total):
            hold[h, part, n] = total

        return store

    def into_sum(h, start):
        def store(n, total):
            summed[start + n, pl.ds(h * 128, 128), :] = total

        return store

    far2 = {}
    for h in range(2):
        for part, start, d in ((0, 0, 1), (1, 8, 3)):
            dense(h, 2, start, into_out(h, part))
            far2[h, d] = go(
                out2.at[h, part], via2.at[h, part], 12 * h + 6 + part, second_peer[h](d)
            )
    last = []
    for h in range(2):
        for part, start, d in ((2, 8, 1), (3, 0, 3)):
            dense(h, d, start, into_out(h, part))
            last.append(
                go(out2.at[h, part], fin.at[h, part - 2], 12 * h + 6 + part, second_peer[h](d))
            )
    for h in range(2):
        dense(h, 1, 0, into_hold(h, 0))
        dense(h, 3, 8, into_hold(h, 1))
    for h in range(2):
        for part, d in ((0, 1), (1, 3)):
            far2[h, d].wait_recv()

            def merge(n, carry, h=h, part=part):
                both = hold[h, part, n] + via2[h, part, n].astype(F32)
                out2[h, 4 + part, n] = both.astype(BF16)
                return carry

            lax.fori_loop(0, 8, merge, 0)
            last.append(
                go(
                    out2.at[h, 4 + part],
                    fin.at[h, 2 + part],
                    12 * h + 10 + part,
                    second_peer[h](d),
                )
            )
    for h in range(2):
        dense(h, 0, 0, into_sum(h, 0))
        dense(h, 0, 8, into_sum(h, 8))
    arrive(last)
    for h in range(2):
        for start, parts in ((0, (1, 2)), (8, (0, 3))):

            def close(n, carry, h=h, start=start, parts=parts):
                total = summed[start + n, pl.ds(h * 128, 128), :]
                for part in parts:
                    total = total + fin[h, part, n].astype(F32)
                summed[start + n, pl.ds(h * 128, 128), :] = total
                return carry

            lax.fori_loop(0, 8, close, 0)
    for copy in done:
        copy.wait_send()


def sum_terms(
    polar_all, new_time, weight_cols, values, item_gram, lengths, slot_of, lists_y, lists_z
):
    smem = pl.BlockSpec(memory_space=pltpu.SMEM)
    block = (128, 128)
    return pl.pallas_call(
        terms_kernel,
        out_shape=(
            jax.ShapeDtypeStruct((16, 256, 128), F32),
            jax.ShapeDtypeStruct((256, 256), F32),
        ),
        in_specs=[VMEM] * 5 + [smem] * 4,
        out_specs=(VMEM,) * 2,
        scratch_shapes=[
            pltpu.VMEM((64, 256, 128), BF16),
            pltpu.VMEM((2, 4, 32) + block, BF16),
            pltpu.VMEM((2, 4, 32) + block, BF16),
            pltpu.VMEM((2, 2, 16) + block, BF16),
            pltpu.VMEM((2, 2, 8) + block, F32),
            pltpu.VMEM((2, 6, 8) + block, BF16),
            pltpu.VMEM((2, 2, 8) + block, BF16),
            pltpu.VMEM((2, 4, 8) + block, BF16),
            pltpu.VMEM((2,) + block, F32),
            pltpu.SemaphoreType.DMA((24,)),
            pltpu.SemaphoreType.DMA((24,)),
        ],
        compiler_params=pltpu.CompilerParams(collective_id=2, has_side_effects=True),
        name="sum_terms",
    )(polar_all, new_time, weight_cols, values, item_gram, lengths, slot_of, lists_y, lists_z)


def panels_kernel(
    items,
    lists,
    weights,
    values,
    lengths,
    place_of,
    partial,
    inner_inv,
    weight_gram,
    lists_y,
    lists_z,
    all_weights,
    line,
    packed,
    got,
    via,
    term,
    full,
    buf_x,
    buf_y,
    buf_z,
    work,
    gram,
    names_y,
    names_z,
    send_sem,
    recv_sem,
    local_sem,
):
    sems = (send_sem, recv_sem)
    y, z, _, _, item = places()
    done = []

    def go(src, dst, n, peer):
        copy = send(src, dst, send_sem.at[n], recv_sem.at[n], user=peer)
        copy.start()
        done.append(copy)
        return copy

    first, second = (z, y), (y, z)
    first_peer = (functools.partial(z_peer, y, z), functools.partial(y_peer, y, z))
    second_peer = (functools.partial(y_peer, y, z), functools.partial(z_peer, y, z))
    wanted = (names_z, names_y)

    def owner(h, a, b):
        return b * 4 + a if h == 0 else a * 4 + b

    lists_y[y] = lists[...]
    lists_z[z] = lists[...]
    all_weights[y, z] = weights[...]
    greet(y, z, item)
    names = []
    for d in range(1, 4):
        names.append(go(lists, lists_y.at[y], 40 + d, y_peer(y, z, d)))
        names.append(go(lists, lists_z.at[z], 44 + d, z_peer(y, z, d)))
    direct = {}
    for h in range(2):
        for d in (1, 3):
            direct[h, d] = go(
                items.at[:, :, pl.ds(h * 128, 128)],
                line.at[h, second[h]],
                48 + 4 * h + d,
                second_peer[h](d),
            )
    wide = []
    for d in range(1, 4):
        mine = all_weights.at[y, z]
        wide.append(go(mine, mine, 24 + d, y_peer(y, z, d)))
    term[...] = jnp.zeros_like(term)

    def add_term(n, carry):
        tile = items[n]
        dims = (((0,), (0,)), ((), ()))
        term[...] += lax.dot_general(tile, tile, dims, preferred_element_type=F32)
        return carry

    lax.fori_loop(0, 16, add_term, 0)
    step = scatter_start(term, buf_x, sems, 0, item)
    done.extend(step)

    def keep(n, carry):
        for h in range(2):
            line[h, second[h], n] = items[n, :, pl.ds(h * 128, 128)]
        return carry

    lax.fori_loop(0, 16, keep, 0)
    arrive(step)
    step = share_start(buf_y, sems, 8, y, functools.partial(y_peer, y, z), total_of(buf_x, 8))
    done.extend(step)
    arrive(names)
    copies = (
        pltpu.make_async_copy(lists_y, names_y, local_sem.at[0]),
        pltpu.make_async_copy(lists_z, names_z, local_sem.at[1]),
    )
    for copy in copies:
        copy.start()
    arrive(wide)
    arrive(step)
    step = share_start(buf_z, sems, 12, z, functools.partial(z_peer, y, z), total_of(buf_y, 4))
    done.extend(step)
    far_wide = []
    for d in range(1, 4):
        mine = all_weights.at[:, z]
        far_wide.append(go(mine, mine, 28 + d, z_peer(y, z, d)))
    hops = []
    for h in range(2):
        before, after = (second[h] + 3) % 4, (second[h] + 1) % 4
        direct[h, 1].wait_recv()
        block = line.at[h, before, pl.ds(0, 8)]
        hops.append(go(block, block, 48 + 4 * h, second_peer[h](1)))
        direct[h, 3].wait_recv()
        block = line.at[h, after, pl.ds(8, 8)]
        hops.append(go(block, block, 50 + 4 * h, second_peer[h](3)))
    for copy in copies:
        copy.wait()
    arrive(hops)

    def pack(h, d):
        a = (first[h] + d) % 4
        out = got if d == 0 else packed

        def one(q, carry):
            b = q // 8
            inside = wanted[h][a, 0, owner(h, first[h], b) * 8 + q % 8]
            out[h, a, q] = line[h, b, inside]
            return carry

        lax.fori_loop(0, 32, one, 0, unroll=4)
        return a

    far = {}
    for h in range(2):
        a = pack(h, 2)
        far[h, 1] = go(packed.at[h, a, pl.ds(0, 16)], via.at[h, 0], 56 + 6 * h, first_peer[h](1))
        far[h, 3] = go(packed.at[h, a, pl.ds(16, 16)], via.at[h, 1], 57 + 6 * h, first_peer[h](3))
    near = []
    for h in range(2):
        for n, d in ((58, 1), (59, 3)):
            a = pack(h, d)
            near.append(go(packed.at[h, a], got.at[h, first[h]], n + 6 * h, first_peer[h](d)))
    arrive(step)
    step = gather_start(full, sems, 16, item, total_of(buf_z, 4))
    done.extend(step)
    for h in range(2):
        pack(h, 0)
    arrive(far_wide)
    stacked = all_weights[...].reshape(256, 256)
    weight_gram[...] = full_dot(stacked.T, stacked)
    arrive(step)
    gram[...] = full[...] * weight_gram[...]
    invert_first(gram, inner_inv, work)
    for h in range(2):
        before, after = (first[h] + 3) % 4, (first[h] + 1) % 4
        far[h, 1].wait_recv()
        near.append(
            go(via.at[h, 0], got.at[h, before, pl.ds(0, 16)], 60 + 6 * h, first_peer[h](1))
        )
        far[h, 3].wait_recv()
        near.append(
            go(via.at[h, 1], got.at[h, after, pl.ds(16, 16)], 61 + 6 * h, first_peer[h](3))
        )
    invert_second(inner_inv, work)
    arrive(near)
    rows = lax.broadcasted_iota(jnp.int32, (256, 256), 0)

    def one_user(k, carry):
        left, right = [], []
        for s in range(4):
            place = place_of[4 * k + s]
            holder, rank = place // 8, place % 8
            at_y, at_z = holder // 4, holder % 4
            low = got[0, at_z, at_y * 8 + rank]
            high = got[1, at_y, at_z * 8 + rank]
            left.append(values[4 * k + s])
            right.append(jnp.concatenate([low, high], axis=1))
        product = jnp.dot(
            jnp.concatenate(left, axis=1),
            jnp.concatenate(right, axis=0),
            preferred_element_type=F32,
        )
        partial[k] = jnp.where(rows < lengths[k], product, 0.0)
        return carry

    lax.fori_loop(0, 16, one_user, 0)
    for copy in done:
        copy.wait_send()


def project(items, lists, weights, values, lengths, place_of):
    smem = pl.BlockSpec(memory_space=pltpu.SMEM)
    block = (128, 128)
    return pl.pallas_call(
        panels_kernel,
        out_shape=(
            jax.ShapeDtypeStruct((16, 256, 256), F32),
            jax.ShapeDtypeStruct((256, 256), F32),
            jax.ShapeDtypeStruct((256, 256), F32),
            jax.ShapeDtypeStruct((4, 8, 128), jnp.int32),
            jax.ShapeDtypeStruct((4, 8, 128), jnp.int32),
        ),
        in_specs=[VMEM] * 4 + [smem] * 2,
        out_specs=(VMEM,) * 5,
        scratch_shapes=[
            pltpu.VMEM((4, 4, 16, 256), F32),
            pltpu.VMEM((2, 4, 16) + block, BF16),
            pltpu.VMEM((2, 4, 32) + block, BF16),
            pltpu.VMEM((2, 4, 32) + block, BF16),
            pltpu.VMEM((2, 2, 16) + block, BF16),
            pltpu.VMEM((256, 256), F32),
            pltpu.VMEM((256, 256), F32),
            pltpu.VMEM((8, 32, 256), F32),
            pltpu.VMEM((4, 32, 256), F32),
            pltpu.VMEM((4, 32, 256), F32),
            pltpu.VMEM((2,) + block, F32),
            pltpu.VMEM((256, 256), F32),
            pltpu.SMEM((4, 8, 128), jnp.int32),
            pltpu.SMEM((4, 8, 128), jnp.int32),
            pltpu.SemaphoreType.DMA((68,)),
            pltpu.SemaphoreType.DMA((68,)),
            pltpu.SemaphoreType.DMA((2,)),
        ],
        compiler_params=pltpu.CompilerParams(collective_id=0, has_side_effects=True),
        name="project",
    )(items, lists, weights, values, lengths, place_of)


def tile_tables(tiles):
    count = tiles.shape[0]
    owners, inside = tiles // 16, tiles % 16
    order = jnp.arange(count, dtype=jnp.int32)
    same = (owners[:, None] == owners[None, :]) & (order[None, :] < order[:, None])
    rank = jnp.sum(same.astype(jnp.int32), axis=1)
    place = owners * 8 + rank
    hit = place[None, :] == jnp.arange(128, dtype=jnp.int32)[:, None]
    want = jnp.sum(jnp.where(hit, inside[None, :], 0), axis=1)
    slot_of = jnp.sum(jnp.where(hit, order[None, :], 0), axis=1)
    named = tiles[None, :] == jnp.arange(256, dtype=jnp.int32)[:, None]
    rank_of = jnp.sum(jnp.where(named, rank[None, :] + 1, 0), axis=1) - 1
    lists = jnp.concatenate([want, rank_of, jnp.zeros((640,), jnp.int32)]).reshape(8, 128)
    return place, slot_of, lists


def body(tile_values, tile_ids, lengths, user_weights, time_factor, item_factor):
    user_count = lax.axis_size("user")
    item_count = lax.axis_size("item")
    item_pos = lax.axis_index("item")
    users_here, slots_user, time_rows, tile_width = tile_values.shape
    rank_size = time_factor.shape[0]
    tiles_owned = item_factor.shape[0] // tile_width
    slot_count = users_here * slots_user
    share_count = users_here // item_count
    flat_ids = (tile_ids - item_pos * (tiles_owned * user_count)).reshape(slot_count)
    place_of, slot_of, lists = tile_tables(flat_ids)
    values = tile_values.reshape(slot_count, time_rows, tile_width)
    partial, inner_inv, weight_gram, lists_y, lists_z = project(
        item_factor.reshape(tiles_owned, tile_width, rank_size),
        lists,
        user_weights,
        values,
        lengths,
        place_of,
    )
    share_weights = lax.dynamic_slice_in_dim(user_weights, item_pos * share_count, share_count, 0)
    polar_all, slices, new_time, item_gram = middle(
        partial, share_weights[:, None, :], time_factor, inner_inv, weight_gram
    )
    summed, gram_inv = sum_terms(
        polar_all,
        new_time,
        user_weights[:, :, None],
        values,
        item_gram,
        lengths,
        slot_of,
        lists_y,
        lists_z,
    )
    new_items = jnp.einsum("nct,cd->ntd", summed, gram_inv, precision=HIGHEST)
    new_items = new_items.reshape(item_factor.shape)
    return (slices, new_time, new_items)


def solution(mesh):
    in_specs = (
        P("user", "item", None, None),
        P("user", "item"),
        P("user"),
        P("user", None),
        P(),
        P(("item", "user"), None),
    )
    out_specs = (P(("user", "item"), None, None), P(), P(("item", "user"), None))
    return jax.shard_map(body, mesh=mesh, in_specs=in_specs, out_specs=out_specs, check_vma=False)
```
